32 devices in a mesh: dp: 4 (over y, x), blk: 8 (over z, core).
Axes of the slice: x: 2, y: 2, z: 4, core: 2. Of those that a mesh axis runs over, the one named last changes fastest.
Arguments:
- slopes: bfloat16 [512, 32768], P('dp', 'blk'), may hold values from -6 to 6
- weights: bfloat16 [256, 16, 128, 128], P('blk'), may hold values from -0.125 to 0.125
- rows: int32 [256, 16], P('blk'), may hold values from 0 to 255
- live: int32 [256, 16], P('blk'), may hold values 0 or 1
- target: bfloat16 [512, 32768], P('dp', 'blk'), may hold values from -6 to 6
Outputs:
- phase: bfloat16 [512, 32768], P('dp', 'blk')
- weight_grad: bfloat16 [16, 256, 128, 128], P('dp', 'blk')
The draws below stay inside these ranges and needn't reach their ends.
All inputs are finite; a program needn't handle non-finite values. No bound on the sum of `live` on one device may be relied on, other than what follows from the above.
Results may differ from the reference program's by a relative error of at most 0.0047.
Values may be sent and summed in bfloat16 or wider, within the bound.
A program may use at most 192 MiB of HBM per device.

```python
import math
import jax
import jax.numpy as jnp
from jax import lax

BS = 128
S = 32768
P_SIZE = 32768
KB = 16
FRAMES = 512
NSB = 256
NCOL = 256


def set_ends(values, rng, low, top_value):
    index_at = [jax.random.randint(jax.random.fold_in(rng, axis), (), 0, length) for axis, length in enumerate(values.shape)]
    widest = values.shape.index(max(values.shape))
    beside = index_at[:widest] + [(index_at[widest] + 1) % values.shape[widest]] + index_at[widest + 1:]
    return values.at[tuple(index_at)].set(low).at[tuple(beside)].set(top_value)


def shard_levels(key, extent, shards, low, high):
    def one(dim, blocks):
        steps = jax.random.uniform(jax.random.fold_in(jax.random.fold_in(key, 6), dim), (blocks,), jnp.float32, low / len(shards), high / len(shards))
        return jnp.repeat(jnp.exp(steps), extent[dim] // blocks).reshape((-1,) + (1,) * (len(extent) - dim - 1))

    factor_of = one(*shards[0])
    for cut in shards[1:]:
        factor_of = factor_of * one(*cut)
    return factor_of


def scatter_about(rng, dims, width, bound, pieces=(), held_as=jnp.bfloat16):
    result = jax.random.normal(rng, dims, jnp.float32) * width
    if len(pieces) > 0:
        result = shard_levels(rng, dims, pieces, -0.22, 0.18) * result
    return jnp.clip(result, min=-bound, max=bound).astype(held_as)


def setup_inputs(seed: int = 0) -> dict:
    arg_keys = jax.random.split(jax.random.key(seed), 6)
    slopes = scatter_about(arg_keys[0], (FRAMES, S), 1.0, 6.0, ((0, 4), (1, 8)))
    weights = scatter_about(arg_keys[1], (NCOL, KB, BS, BS), (KB * BS) ** -0.5, 0.125, ((0, 8),))
    rows = set_ends(jax.random.randint(arg_keys[2], (NCOL, KB), 0, NSB), jax.random.fold_in(arg_keys[2], 1), 0, NSB - 1).astype(jnp.int32)
    live = set_ends((jax.random.randint(arg_keys[3], (NCOL, KB), 0, 4) < 3).astype(jnp.int32), jax.random.fold_in(arg_keys[3], 1), 0, 1)
    target = scatter_about(arg_keys[4], (FRAMES, P_SIZE), 1.0, 6.0, ((0, 4), (1, 8)))
    return {"slopes": slopes, "weights": weights, "rows": rows, "live": live, "target": target}


def reference(slopes, weights, rows, live, target):
    slope_tiles = slopes.reshape(FRAMES, NSB, BS)
    live_float = live.astype(jnp.float32)

    def forward(packed):
        weight_col, row_col, live_col = packed
        tiles = jnp.take(slope_tiles, row_col.astype(jnp.int32), axis=1).astype(jnp.float32)
        return jnp.einsum('fkb,kbc,k->fc', tiles, weight_col.astype(jnp.float32), live_col)
    outputs = lax.map(forward, (weights, rows, live_float))
    predicted = jnp.transpose(outputs, (1, 0, 2)).reshape(FRAMES, P_SIZE)
    phase = predicted.astype(jnp.bfloat16)
    errors = ((predicted - target.astype(jnp.float32)) * (1.0 / math.sqrt(FRAMES))).astype(jnp.bfloat16)
    error_cols = jnp.transpose(errors.reshape(FRAMES, NCOL, BS), (1, 0, 2))

    def backward(packed):
        row_col, live_col, err_col = packed
        tiles = jnp.take(slope_tiles, row_col.astype(jnp.int32), axis=1).astype(jnp.float32)
        return jnp.einsum('fkb,fc,k->kbc', tiles, err_col.astype(jnp.float32), live_col)
    grads = lax.map(backward, (rows, live_float, error_cols))
    return (phase, jnp.transpose(grads, (1, 0, 2, 3)).astype(jnp.bfloat16))
```

```python
import functools
import math

import jax
import jax.numpy as jnp
from jax import lax
from jax.experimental import pallas as pl
from jax.experimental.pallas import tpu as pltpu
from jax.sharding import PartitionSpec as P

MESH = pl.DeviceIdType.MESH
VMEM_BYTES = 64 << 20
SLOTS = 4
PARTS = 4
PIECES = 8


def fused_kernel(
    depth_z, slopes, weights, target, rows, live, phase, sums, dline, ed,
    own, xline, yline, turned, e0, ex, ey, wbuf, tbuf, load_sem, w_sem, t_sem,
    up_send, down_send, z_recv, x_send, x_recv, y_send, y_recv, d_send, d_recv,
    s_send, s_recv, ex_send, ex_recv, ey_send, ey_recv, ed_send, ed_recv,
):
    depth, columns = rows.shape
    size = own.shape[1]
    frames = own.shape[1]
    per = slopes.shape[1] // own.shape[2]
    half = per // PARTS
    half_cols = columns // 2
    p = lax.axis_index("dp")
    b = lax.axis_index("blk")
    z, core = b // 2, b % 2
    sib = b + 1 - 2 * core
    across = (p + 1 - 2 * (p % 2), b)
    along = ((p + 2) % 4, b)
    beside = (p, sib)
    total_frames = 4 * frames

    lines = (own, xline, yline, dline)

    def chunk(line, zz, cc, h):
        return line.at[pl.ds((zz * 2 + cc) * per + h * half, half)]

    def remote(src, dst, send, recv, to):
        return pltpu.make_async_remote_copy(
            src_ref=src, dst_ref=dst, send_sem=send, recv_sem=recv, device_id=to, device_id_type=MESH
        )

    def up(n, zz, h):
        c = chunk(lines[n], zz, core, h)
        return remote(c, c, up_send.at[n // 3, zz, h], z_recv.at[n // 3, zz, h], (p, b + 2))

    def down(n, zz, h):
        c = chunk(lines[n], zz, core, h)
        return remote(c, c, down_send.at[n // 3, zz, h], z_recv.at[n // 3, zz, h], (p, b - 2))

    def over_x(zz, h):
        return remote(chunk(own, zz, core, h), chunk(xline, zz, core, h), x_send.at[zz, h], x_recv.at[zz, h], across)

    def over_y(zz, h):
        return remote(chunk(own, zz, core, h), chunk(yline, zz, core, h), y_send.at[zz, h], y_recv.at[zz, h], along)

    def diagonal(zz, h):
        to = (across, along)[h % 2]
        source = turned.at[pl.ds(h * half, half)]
        return remote(source, chunk(dline, zz, core, h), d_send.at[zz, h], d_recv.at[zz, h], to)

    def turn(zz, h):
        source = (yline, xline)[h % 2]

        def one(i, carry):
            turned[h * half + i] = source[(zz * 2 + core) * per + h * half + i].T
            return carry

        lax.fori_loop(0, half, one, 0)

    def share(n, zz, h):
        c = chunk(lines[n], zz, core, h)
        return remote(c, c, s_send.at[n, zz, h], s_recv.at[n, zz, h], beside)

    def shared(n, zz, h):
        c = chunk(lines[n], zz, 1 - core, h)
        return remote(c, c, s_send.at[n, zz, h], s_recv.at[n, zz, h], beside)

    def error_part(ref, h):
        return ref.at[pl.ds(h * half_cols, half_cols)]

    def errors_x(h):
        return remote(error_part(e0, h), error_part(ex, h), ex_send.at[h], ex_recv.at[h], across)

    def errors_y(h):
        return remote(error_part(e0, h), error_part(ey, h), ey_send.at[h], ey_recv.at[h], along)

    def errors_d(h):
        source, to = ((ey, across), (ex, along))[h]
        return remote(error_part(source, h), error_part(ed, h), ed_send.at[h], ed_recv.at[h], to)

    def load_weights(j):
        slot = j % SLOTS
        return pltpu.make_async_copy(weights.at[j], wbuf.at[slot], w_sem.at[slot])

    def load_target():
        return pltpu.make_async_copy(target, tbuf, t_sem)

    for i in range(per):
        pltpu.make_async_copy(
            slopes.at[:, pl.ds(i * size, size)], own.at[b * per + i], load_sem.at[i // half]
        ).start()

    barrier = pltpu.get_barrier_semaphore()
    for to in (across, along, beside):
        pl.semaphore_signal(barrier, inc=1, device_id=to, device_id_type=MESH)

    @pl.when(z > 0)
    def _():
        pl.semaphore_signal(barrier, inc=1, device_id=(p, b - 2), device_id_type=MESH)

    @pl.when(z < depth_z - 1)
    def _():
        pl.semaphore_signal(barrier, inc=1, device_id=(p, b + 2), device_id_type=MESH)

    pl.semaphore_wait(barrier, 3 + jnp.minimum(z, 1) + jnp.minimum(depth_z - 1 - z, 1))

    def at_distance(s, act):
        if s == 0:
            act(z, True, True)
            return

        @pl.when(z - s >= 0)
        def _():
            act(z - s, True, False)

        @pl.when(z + s < depth_z)
        def _():
            act(z + s, False, True)

    def relay(n, zz, h, upward, downward):
        if upward:
            @pl.when(z < depth_z - 1)
            def _():
                up(n, zz, h).start()
        if downward:
            @pl.when(z > 0)
            def _():
                down(n, zz, h).start()

    def send_own(s, h):
        def act(zz, upward, downward):
            if s > 0:
                (up if upward else down)(0, zz, h).wait_recv()
            relay(0, zz, h, upward, downward)
            share(0, zz, h).start()

        def spread(zz, upward, downward):
            over_x(zz, h).start()
            over_y(zz, h).start()

        at_distance(s, act)
        if s == 1:
            pass_on(0, h)
        at_distance(s, spread)

    def send_diagonal(s, h, inner):
        def act(zz, upward, downward):
            if s == 0:
                diagonal(zz, h).wait_recv()
            else:
                (up if upward else down)(3, zz, h).wait_recv()
            relay(3, zz, h, upward, downward)
            share(3, zz, h).start()

        def guarded(zz, upward, downward):
            ends = z < depth_z - 1 if upward else z > 0

            @pl.when(ends if inner else jnp.logical_not(ends))
            def _():
                act(zz, upward, downward)

        at_distance(s, act if s == 0 else guarded)

    def pass_on(s, h):
        def act(zz, upward, downward):
            over_x(zz, h).wait_recv()
            over_y(zz, h).wait_recv()
            if s == 0:
                turn(zz, h)
                diagonal(zz, h).start()
            share(1, zz, h).start()
            share(2, zz, h).start()

        at_distance(s, act)

    for h in range(PARTS):
        pltpu.make_async_copy(chunk(own, z, core, h), chunk(own, z, core, h), load_sem.at[h]).wait()
        send_own(0, h)
    load_target().start()
    for j in range(SLOTS):
        load_weights(j).start()
    for s in range(1, depth_z):
        if s == depth_z - 1:
            for h in range(PARTS):
                send_diagonal(0, h, True)
        for h in range(PARTS):
            send_own(s, h)

    for zz in range(depth_z):
        for h in range(PARTS):
            shared(0, zz, h).wait_recv()
    load_target().wait()

    def forward(j, carry):
        load_weights(j).wait()
        slot = j % SLOTS
        picked, masked = [], []
        for k in range(depth):
            picked.append(own[rows[k, j]])
            keep = jnp.full((size, size), live[k, j].astype(jnp.float32), jnp.float32).astype(jnp.bfloat16)
            masked.append(wbuf[slot, k] * keep)
        predicted = jnp.dot(
            jnp.concatenate(picked, 1), jnp.concatenate(masked, 0), preferred_element_type=jnp.float32
        )
        where = pl.ds(pl.multiple_of(j * size, size), size)
        phase[:, where] = predicted.astype(jnp.bfloat16)
        off = predicted - tbuf[:, where].astype(jnp.float32)
        e0[j] = (off * (1.0 / math.sqrt(total_frames))).astype(jnp.bfloat16)

        @pl.when(j + SLOTS < columns)
        def _():
            load_weights(j + SLOTS).start()

        return carry

    lax.fori_loop(0, columns, forward, 0)
    for h in range(2):
        errors_x(1 - h).start()
        errors_y(h).start()

    for s in range(1, depth_z):
        for h in range(PARTS):
            send_diagonal(s, h, True)
    for s in range(1, depth_z):
        for h in range(PARTS):
            pass_on(s, h)
    for s in range(1, depth_z - 1):
        if s == depth_z - 2:
            errors_y(0).wait_recv()
            errors_d(0).start()
            errors_x(1).wait_recv()
            errors_d(1).start()
        for h in range(PARTS):
            send_diagonal(s, h, False)
    errors_x(0).wait_recv()
    errors_y(1).wait_recv()
    for n in range(1, 3):
        for zz in range(depth_z):
            for h in range(PARTS):
                shared(n, zz, h).wait_recv()

    count = sums.shape[1] // size

    def near(j, carry):
        tiles = []
        for i in range(count):
            r = rows[p * count + i, j]
            tiles.append(jnp.concatenate([line[r] for line in (own, xline, yline)], 0))
        left = jnp.concatenate([e[j].T for e in (e0, ex, ey)], 1)
        both = jnp.dot(left, jnp.concatenate(tiles, 1), preferred_element_type=jnp.float32)
        for i in range(count):
            sums[j, pl.ds(i * size, size)] = both[:, i * size : (i + 1) * size].T
        return carry

    lax.fori_loop(0, columns, near, 0)

    def sent(lines_sent, ends):
        for h in range(PARTS):
            for s in range(depth_z):
                def done(zz, upward, downward, h=h, s=s):
                    for n in lines_sent:
                        if upward and n % 3 == 0:
                            @pl.when(z < depth_z - 1)
                            def _(n=n):
                                up(n, zz, h).wait_send()
                        if downward and n % 3 == 0:
                            @pl.when(z > 0)
                            def _(n=n):
                                down(n, zz, h).wait_send()
                        share(n, zz, h).wait_send()
                    if not ends:
                        over_x(zz, h).wait_send()
                        over_y(zz, h).wait_send()
                        if s == 0:
                            diagonal(zz, h).wait_send()

                at_distance(s, done)

    sent((0, 1, 2), False)
    for h in range(PARTS):
        send_diagonal(depth_z - 1, h, False)
    for h in range(2):
        errors_x(h).wait_send()
        errors_y(h).wait_send()
        errors_d(h).wait_send()
        errors_d(h).wait_recv()
    for zz in range(depth_z):
        for h in range(PARTS):
            shared(3, zz, h).wait_recv()
    sent((3,), True)


def finish_kernel(phase, sums, dline, ed, rows, live, phase_out, grads_out, grads, phase_sem, grads_sem):
    columns, size, _ = ed.shape
    count = grads.shape[0]
    first = lax.axis_index("dp") * count
    pieces = grads_sem.shape[0]
    part = columns // pieces
    put = [pltpu.make_async_copy(phase, phase_out, phase_sem)]
    put[0].start()

    def far(j, carry):
        left = jnp.concatenate([dline[rows[first + i, j]] for i in range(count)], 0)
        both = sums[j] + jnp.dot(left, ed[j], preferred_element_type=jnp.float32)
        for i in range(count):
            keep = live[first + i, j].astype(jnp.float32)
            grads[i, j] = (both[i * size : (i + 1) * size] * keep).astype(jnp.bfloat16)
        return carry

    for q in range(pieces):
        lax.fori_loop(q * part, (q + 1) * part, far, 0)
        for i in range(count):
            where = (i, pl.ds(q * part, part))
            put.append(pltpu.make_async_copy(grads.at[where], grads_out.at[where], grads_sem.at[q, i]))
            put[-1].start()
    for copy in put:
        copy.wait()


def fused(slopes, weights, rows, live, target):
    frames = slopes.shape[0]
    columns, depth, size, _ = weights.shape
    blk = lax.axis_size("blk")
    depth_z = blk // 2
    blocks = slopes.shape[1] * blk // size
    count = depth // 4
    line = pltpu.VMEM((blocks, frames, size), jnp.bfloat16)
    errors = pltpu.VMEM((columns, frames, size), jnp.bfloat16)
    dma = pltpu.SemaphoreType.DMA
    everywhere = pl.BlockSpec(memory_space=pl.ANY)
    smem = pl.BlockSpec(memory_space=pltpu.SMEM)
    vmem = pl.BlockSpec(memory_space=pltpu.VMEM)
    slopes, weights, target = (pltpu.with_memory_space_constraint(a, pltpu.HBM) for a in (slopes, weights, target))
    handed = pl.pallas_call(
        functools.partial(fused_kernel, depth_z),
        out_shape=(
            pltpu.VMEM(target.shape, jnp.bfloat16),
            pltpu.VMEM((columns, count * size, size), jnp.float32),
            line,
            errors,
        ),
        in_specs=[everywhere, everywhere, everywhere, smem, smem],
        out_specs=(vmem,) * 4,
        scratch_shapes=[line] * 3
        + [pltpu.VMEM((blocks // blk, size, frames), jnp.bfloat16)]
        + [errors] * 3
        + [pltpu.VMEM((SLOTS, depth, size, size), jnp.bfloat16), pltpu.VMEM(target.shape, jnp.bfloat16)]
        + [dma((PARTS,)), dma((SLOTS,)), dma]
        + [dma((2, depth_z, PARTS))] * 3
        + [dma((depth_z, PARTS))] * 6
        + [dma((4, depth_z, PARTS))] * 2
        + [dma((2,))] * 6,
        compiler_params=pltpu.CompilerParams(
            collective_id=0, has_side_effects=True, vmem_limit_bytes=VMEM_BYTES * 5 // 8
        ),
    )(slopes, weights, target, rows.T, live.T)
    handed = [pltpu.with_memory_space_constraint(a, pltpu.VMEM) for a in handed]
    grads = (count, columns, size, size)
    return pl.pallas_call(
        finish_kernel,
        out_shape=(jax.ShapeDtypeStruct(target.shape, jnp.bfloat16), jax.ShapeDtypeStruct(grads, jnp.bfloat16)),
        in_specs=[vmem] * 4 + [smem] * 2,
        out_specs=(everywhere,) * 2,
        scratch_shapes=[pltpu.VMEM(grads, jnp.bfloat16), dma, dma((PIECES, count))],
        compiler_params=pltpu.CompilerParams(vmem_limit_bytes=VMEM_BYTES // 4),
    )(*handed, rows.T, live.T)


def gathered_step(slopes, weights, rows, live, target):
    own = lax.all_gather(slopes, "blk", axis=1, tiled=True)
    everyone = lax.all_gather(own, "dp", axis=0, tiled=True)
    frames = own.shape[0]
    columns, depth, size, _ = weights.shape
    dp = lax.axis_size("dp")
    share = depth // dp
    total_frames = frames * dp

    def tiles(lines, some):
        return [lax.dynamic_slice_in_dim(lines, some[k] * size, size, 1) for k in range(some.shape[0])]

    def forward(column):
        blocks, some, seen = column
        masked = blocks * seen.astype(jnp.bfloat16)[:, None, None]
        return jnp.dot(
            jnp.concatenate(tiles(own, some), 1), masked.reshape(-1, size), preferred_element_type=jnp.float32
        )

    predicted = jnp.transpose(lax.map(forward, (weights, rows, live)), (1, 0, 2)).reshape(frames, -1)
    errors = ((predicted - target.astype(jnp.float32)) * (1.0 / math.sqrt(total_frames))).astype(jnp.bfloat16)
    errors = lax.all_gather(errors, "dp", axis=0, tiled=True)
    first = lax.axis_index("dp") * share

    def backward(column):
        j, some, seen = column
        left = jnp.concatenate(tiles(everyone, some), 1)
        right = lax.dynamic_slice_in_dim(errors, j * size, size, 1)
        grads = lax.dot_general(left, right, (((0,), (0,)), ((), ())), preferred_element_type=jnp.float32)
        return (grads.reshape(share, size, size) * seen.astype(jnp.float32)[:, None, None]).astype(jnp.bfloat16)

    mine = [lax.dynamic_slice_in_dim(a, first, share, 1) for a in (rows, live)]
    grads = lax.map(backward, (jnp.arange(columns), *mine))
    return predicted.astype(jnp.bfloat16), jnp.transpose(grads, (1, 0, 2, 3))


def on_device(slopes, weights, rows, live, target):
    dp, blk = lax.axis_size("dp"), lax.axis_size("blk")
    held = 2 * dp * slopes.size * blk + 6 * target.size * dp
    if dp == 4 and blk == 8 and slopes.shape[0] == weights.shape[2] and held < VMEM_BYTES * 3 // 4:
        return fused(slopes, weights, rows, live, target)
    return gathered_step(slopes, weights, rows, live, target)


def solution(mesh):
    return jax.shard_map(
        on_device,
        mesh=mesh,
        in_specs=(
            P("dp", "blk"),
            P("blk", None, None, None),
            P("blk", None),
            P("blk", None),
            P("dp", "blk"),
        ),
        out_specs=(P("dp", "blk"), P("dp", "blk", None, None)),
        check_vma=False,
    )
```

```python
import functools
import math

import jax
import jax.numpy as jnp
from jax import lax
from jax.experimental import pallas as pl
from jax.experimental.pallas import tpu as pltpu
from jax.sharding import PartitionSpec as P

MESH = pl.DeviceIdType.MESH
VMEM_BYTES = 64 << 20
SLOTS = 4
PARTS = 2
PIECES = 8


def fused_kernel(
    depth_z, slopes, weights, target, rows, live, phase, sums, dline, ed,
    own, xline, yline, turned, e0, ex, ey, wbuf, tbuf, load_sem, w_sem, t_sem,
    up_send, down_send, z_recv, x_send, x_recv, y_send, y_recv, d_send, d_recv,
    s_send, s_recv, ex_send, ex_recv, ey_send, ey_recv, ed_send, ed_recv,
):
    depth, columns = rows.shape
    size = own.shape[1]
    frames = own.shape[1]
    per = slopes.shape[1] // own.shape[2]
    half = per // PARTS
    half_cols = columns // 2
    p = lax.axis_index("dp")
    b = lax.axis_index("blk")
    z, core = b // 2, b % 2
    sib = b + 1 - 2 * core
    across = (p + 1 - 2 * (p % 2), b)
    along = ((p + 2) % 4, b)
    beside = (p, sib)
    total_frames = 4 * frames

    lines = (own, xline, yline, dline)

    def chunk(line, zz, cc, h):
        return line.at[pl.ds((zz * 2 + cc) * per + h * half, half)]

    def remote(src, dst, send, recv, to):
        return pltpu.make_async_remote_copy(
            src_ref=src, dst_ref=dst, send_sem=send, recv_sem=recv, device_id=to, device_id_type=MESH
        )

    def up(n, zz, h):
        c = chunk(lines[n], zz, core, h)
        return remote(c, c, up_send.at[n // 3, zz, h], z_recv.at[n // 3, zz, h], (p, b + 2))

    def down(n, zz, h):
        c = chunk(lines[n], zz, core, h)
        return remote(c, c, down_send.at[n // 3, zz, h], z_recv.at[n // 3, zz, h], (p, b - 2))

    def over_x(zz, h):
        return remote(chunk(own, zz, core, h), chunk(xline, zz, core, h), x_send.at[zz, h], x_recv.at[zz, h], across)

    def over_y(zz, h):
        return remote(chunk(own, zz, core, h), chunk(yline, zz, core, h), y_send.at[zz, h], y_recv.at[zz, h], along)

    def diagonal(zz, h):
        to = (across, along)[h % 2]
        source = turned.at[pl.ds(h * half, half)]
        return remote(source, chunk(dline, zz, core, h), d_send.at[zz, h], d_recv.at[zz, h], to)

    def turn(zz, h):
        source = (yline, xline)[h % 2]

        def one(i, carry):
            turned[h * half + i] = source[(zz * 2 + core) * per + h * half + i].T
            return carry

        lax.fori_loop(0, half, one, 0)

    def share(n, zz, h):
        c = chunk(lines[n], zz, core, h)
        return remote(c, c, s_send.at[n, zz, h], s_recv.at[n, zz, h], beside)

    def shared(n, zz, h):
        c = chunk(lines[n], zz, 1 - core, h)
        return remote(c, c, s_send.at[n, zz, h], s_recv.at[n, zz, h], beside)

    def error_part(ref, h):
        return ref.at[pl.ds(h * half_cols, half_cols)]

    def errors_x(h):
        return remote(error_part(e0, h), error_part(ex, h), ex_send.at[h], ex_recv.at[h], across)

    def errors_y(h):
        return remote(error_part(e0, h), error_part(ey, h), ey_send.at[h], ey_recv.at[h], along)

    def errors_d(h):
        source, to = ((ey, across), (ex, along))[h]
        return remote(error_part(source, h), error_part(ed, h), ed_send.at[h], ed_recv.at[h], to)

    def load_weights(j):
        slot = j % SLOTS
        return pltpu.make_async_copy(weights.at[j], wbuf.at[slot], w_sem.at[slot])

    def load_target():
        return pltpu.make_async_copy(target, tbuf, t_sem)

    for i in range(per):
        pltpu.make_async_copy(
            slopes.at[:, pl.ds(i * size, size)], own.at[b * per + i], load_sem.at[i // half]
        ).start()

    barrier = pltpu.get_barrier_semaphore()
    for to in (across, along, beside):
        pl.semaphore_signal(barrier, inc=1, device_id=to, device_id_type=MESH)

    @pl.when(z > 0)
    def _():
        pl.semaphore_signal(barrier, inc=1, device_id=(p, b - 2), device_id_type=MESH)

    @pl.when(z < depth_z - 1)
    def _():
        pl.semaphore_signal(barrier, inc=1, device_id=(p, b + 2), device_id_type=MESH)

    pl.semaphore_wait(barrier, 3 + jnp.minimum(z, 1) + jnp.minimum(depth_z - 1 - z, 1))

    def at_distance(s, act):
        if s == 0:
            act(z, True, True)
            return

        @pl.when(z - s >= 0)
        def _():
            act(z - s, True, False)

        @pl.when(z + s < depth_z)
        def _():
            act(z + s, False, True)

    def relay(n, zz, h, upward, downward):
        if upward:
            @pl.when(z < depth_z - 1)
            def _():
                up(n, zz, h).start()
        if downward:
            @pl.when(z > 0)
            def _():
                down(n, zz, h).start()

    def send_own(s, h):
        def act(zz, upward, downward):
            if s > 0:
                (up if upward else down)(0, zz, h).wait_recv()
            relay(0, zz, h, upward, downward)
            share(0, zz, h).start()

        def spread(zz, upward, downward):
            over_x(zz, h).start()
            over_y(zz, h).start()

        at_distance(s, act)
        if s == 1:
            pass_on(0, h)
        at_distance(s, spread)

    def send_diagonal(s, h, inner):
        def act(zz, upward, downward):
            if s == 0:
                diagonal(zz, h).wait_recv()
            else:
                (up if upward else down)(3, zz, h).wait_recv()
            relay(3, zz, h, upward, downward)
            share(3, zz, h).start()

        def guarded(zz, upward, downward):
            ends = z < depth_z - 1 if upward else z > 0

            @pl.when(ends if inner else jnp.logical_not(ends))
            def _():
                act(zz, upward, downward)

        at_distance(s, act if s == 0 else guarded)

    def pass_on(s, h):
        def act(zz, upward, downward):
            over_x(zz, h).wait_recv()
            over_y(zz, h).wait_recv()
            if s == 0:
                turn(zz, h)
                diagonal(zz, h).start()
            share(1, zz, h).start()
            share(2, zz, h).start()

        at_distance(s, act)

    for h in range(PARTS):
        pltpu.make_async_copy(chunk(own, z, core, h), chunk(own, z, core, h), load_sem.at[h]).wait()
        send_own(0, h)
    load_target().start()
    for j in range(SLOTS):
        load_weights(j).start()
    for s in range(1, depth_z):
        if s == depth_z - 1:
            for h in range(PARTS):
                send_diagonal(0, h, True)
        for h in range(PARTS):
            send_own(s, h)

    for zz in range(depth_z):
        for h in range(PARTS):
            shared(0, zz, h).wait_recv()
    load_target().wait()

    def forward(j, carry):
        load_weights(j).wait()
        slot = j % SLOTS
        picked, masked = [], []
        for k in range(depth):
            picked.append(own[rows[k, j]])
            keep = jnp.full((size, size), live[k, j].astype(jnp.float32), jnp.float32).astype(jnp.bfloat16)
            masked.append(wbuf[slot, k] * keep)
        predicted = jnp.dot(
            jnp.concatenate(picked, 1), jnp.concatenate(masked, 0), preferred_element_type=jnp.float32
        )
        where = pl.ds(pl.multiple_of(j * size, size), size)
        phase[:, where] = predicted.astype(jnp.bfloat16)
        off = predicted - tbuf[:, where].astype(jnp.float32)
        e0[j] = (off * (1.0 / math.sqrt(total_frames))).astype(jnp.bfloat16)

        @pl.when(j + SLOTS < columns)
        def _():
            load_weights(j + SLOTS).start()

        return carry

    lax.fori_loop(0, columns, forward, 0)
    for h in range(2):
        errors_x(1 - h).start()
        errors_y(h).start()

    for s in range(1, depth_z):
        for h in range(PARTS):
            send_diagonal(s, h, True)
    for s in range(1, depth_z):
        for h in range(PARTS):
            pass_on(s, h)
    for s in range(1, depth_z - 1):
        if s == depth_z - 2:
            errors_y(0).wait_recv()
            errors_d(0).start()
            errors_x(1).wait_recv()
            errors_d(1).start()
        for h in range(PARTS):
            send_diagonal(s, h, False)
    errors_x(0).wait_recv()
    errors_y(1).wait_recv()
    for n in range(1, 3):
        for zz in range(depth_z):
            for h in range(PARTS):
                shared(n, zz, h).wait_recv()

    count = sums.shape[1] // size

    def near(j, carry):
        tiles = []
        for i in range(count):
            r = rows[p * count + i, j]
            tiles.append(jnp.concatenate([line[r] for line in (own, xline, yline)], 0))
        left = jnp.concatenate([e[j].T for e in (e0, ex, ey)], 1)
        both = jnp.dot(left, jnp.concatenate(tiles, 1), preferred_element_type=jnp.float32)
        for i in range(count):
            sums[j, pl.ds(i * size, size)] = both[:, i * size : (i + 1) * size].T
        return carry

    lax.fori_loop(0, columns, near, 0, unroll=2)

    def sent(lines_sent, ends):
        for h in range(PARTS):
            for s in range(depth_z):
                def done(zz, upward, downward, h=h, s=s):
                    for n in lines_sent:
                        if upward and n % 3 == 0:
                            @pl.when(z < depth_z - 1)
                            def _(n=n):
                                up(n, zz, h).wait_send()
                        if downward and n % 3 == 0:
                            @pl.when(z > 0)
                            def _(n=n):
                                down(n, zz, h).wait_send()
                        share(n, zz, h).wait_send()
                    if not ends:
                        over_x(zz, h).wait_send()
                        over_y(zz, h).wait_send()
                        if s == 0:
                            diagonal(zz, h).wait_send()

                at_distance(s, done)

    sent((0, 1, 2), False)
    for h in range(PARTS):
        send_diagonal(depth_z - 1, h, False)
    for h in range(2):
        errors_x(h).wait_send()
        errors_y(h).wait_send()
        errors_d(h).wait_send()
        errors_d(h).wait_recv()
    for zz in range(depth_z):
        for h in range(PARTS):
            shared(3, zz, h).wait_recv()
    sent((3,), True)


def finish_kernel(phase, sums, dline, ed, rows, live, phase_out, grads_out, grads, phase_sem, grads_sem):
    columns, size, _ = ed.shape
    count = grads.shape[0]
    first = lax.axis_index("dp") * count
    pieces = grads_sem.shape[0]
    part = columns // pieces
    put = [pltpu.make_async_copy(phase, phase_out, phase_sem)]
    put[0].start()

    def far(j, carry):
        left = jnp.concatenate([dline[rows[first + i, j]] for i in range(count)], 0)
        both = sums[j] + jnp.dot(left, ed[j], preferred_element_type=jnp.float32)
        for i in range(count):
            keep = live[first + i, j].astype(jnp.float32)
            grads[i, j] = (both[i * size : (i + 1) * size] * keep).astype(jnp.bfloat16)
        return carry

    for q in range(pieces):
        lax.fori_loop(q * part, (q + 1) * part, far, 0, unroll=4)
        for i in range(count):
            where = (i, pl.ds(q * part, part))
            put.append(pltpu.make_async_copy(grads.at[where], grads_out.at[where], grads_sem.at[q, i]))
            put[-1].start()
    for copy in put:
        copy.wait()


def fused(slopes, weights, rows, live, target):
    frames = slopes.shape[0]
    columns, depth, size, _ = weights.shape
    blk = lax.axis_size("blk")
    depth_z = blk // 2
    blocks = slopes.shape[1] * blk // size
    count = depth // 4
    line = pltpu.VMEM((blocks, frames, size), jnp.bfloat16)
    errors = pltpu.VMEM((columns, frames, size), jnp.bfloat16)
    dma = pltpu.SemaphoreType.DMA
    everywhere = pl.BlockSpec(memory_space=pl.ANY)
    smem = pl.BlockSpec(memory_space=pltpu.SMEM)
    vmem = pl.BlockSpec(memory_space=pltpu.VMEM)
    slopes, weights, target = (pltpu.with_memory_space_constraint(a, pltpu.HBM) for a in (slopes, weights, target))
    handed = pl.pallas_call(
        functools.partial(fused_kernel, depth_z),
        out_shape=(
            pltpu.VMEM(target.shape, jnp.bfloat16),
            pltpu.VMEM((columns, count * size, size), jnp.float32),
            line,
            errors,
        ),
        in_specs=[everywhere, everywhere, everywhere, smem, smem],
        out_specs=(vmem,) * 4,
        scratch_shapes=[line] * 3
        + [pltpu.VMEM((blocks // blk, size, frames), jnp.bfloat16)]
        + [errors] * 3
        + [pltpu.VMEM((SLOTS, depth, size, size), jnp.bfloat16), pltpu.VMEM(target.shape, jnp.bfloat16)]
        + [dma((PARTS,)), dma((SLOTS,)), dma]
        + [dma((2, depth_z, PARTS))] * 3
        + [dma((depth_z, PARTS))] * 6
        + [dma((4, depth_z, PARTS))] * 2
        + [dma((2,))] * 6,
        compiler_params=pltpu.CompilerParams(
            collective_id=0, has_side_effects=True, vmem_limit_bytes=VMEM_BYTES * 5 // 8
        ),
    )(slopes, weights, target, rows.T, live.T)
    handed = [pltpu.with_memory_space_constraint(a, pltpu.VMEM) for a in handed]
    grads = (count, columns, size, size)
    return pl.pallas_call(
        finish_kernel,
        out_shape=(jax.ShapeDtypeStruct(target.shape, jnp.bfloat16), jax.ShapeDtypeStruct(grads, jnp.bfloat16)),
        in_specs=[vmem] * 4 + [smem] * 2,
        out_specs=(everywhere,) * 2,
        scratch_shapes=[pltpu.VMEM(grads, jnp.bfloat16), dma, dma((PIECES, count))],
        compiler_params=pltpu.CompilerParams(vmem_limit_bytes=VMEM_BYTES // 4),
    )(*handed, rows.T, live.T)


def gathered_step(slopes, weights, rows, live, target):
    own = lax.all_gather(slopes, "blk", axis=1, tiled=True)
    everyone = lax.all_gather(own, "dp", axis=0, tiled=True)
    frames = own.shape[0]
    columns, depth, size, _ = weights.shape
    dp = lax.axis_size("dp")
    share = depth // dp
    total_frames = frames * dp

    def tiles(lines, some):
        return [lax.dynamic_slice_in_dim(lines, some[k] * size, size, 1) for k in range(some.shape[0])]

    def forward(column):
        blocks, some, seen = column
        masked = blocks * seen.astype(jnp.bfloat16)[:, None, None]
        return jnp.dot(
            jnp.concatenate(tiles(own, some), 1), masked.reshape(-1, size), preferred_element_type=jnp.float32
        )

    predicted = jnp.transpose(lax.map(forward, (weights, rows, live)), (1, 0, 2)).reshape(frames, -1)
    errors = ((predicted - target.astype(jnp.float32)) * (1.0 / math.sqrt(total_frames))).astype(jnp.bfloat16)
    errors = lax.all_gather(errors, "dp", axis=0, tiled=True)
    first = lax.axis_index("dp") * share

    def backward(column):
        j, some, seen = column
        left = jnp.concatenate(tiles(everyone, some), 1)
        right = lax.dynamic_slice_in_dim(errors, j * size, size, 1)
        grads = lax.dot_general(left, right, (((0,), (0,)), ((), ())), preferred_element_type=jnp.float32)
        return (grads.reshape(share, size, size) * seen.astype(jnp.float32)[:, None, None]).astype(jnp.bfloat16)

    mine = [lax.dynamic_slice_in_dim(a, first, share, 1) for a in (rows, live)]
    grads = lax.map(backward, (jnp.arange(columns), *mine))
    return predicted.astype(jnp.bfloat16), jnp.transpose(grads, (1, 0, 2, 3))


def on_device(slopes, weights, rows, live, target):
    dp, blk = lax.axis_size("dp"), lax.axis_size("blk")
    held = 2 * dp * slopes.size * blk + 6 * target.size * dp
    if dp == 4 and blk == 8 and slopes.shape[0] == weights.shape[2] and held < VMEM_BYTES * 3 // 4:
        return fused(slopes, weights, rows, live, target)
    return gathered_step(slopes, weights, rows, live, target)


def solution(mesh):
    return jax.shard_map(
        on_device,
        mesh=mesh,
        in_specs=(
            P("dp", "blk"),
            P("blk", None, None, None),
            P("blk", None),
            P("blk", None),
            P("dp", "blk"),
        ),
        out_specs=(P("dp", "blk"), P("dp", "blk", None, None)),
        check_vma=False,
    )
```

```python
import functools
import math

import jax
import jax.numpy as jnp
from jax import lax
from jax.experimental import pallas as pl
from jax.experimental.pallas import tpu as pltpu
from jax.sharding import PartitionSpec as P

MESH = pl.DeviceIdType.MESH
VMEM_BYTES = 64 << 20
SLOTS = 4
PARTS = 2
TAIL = 2
PIECES = 8


def fused_kernel(
    depth_z, slopes, weights, target, rows_in, live_in, phase, sums, dline, ed, rows, live,
    own, xline, yline, turned, e0, ex, ey, wbuf, tbuf, load_sem, w_sem, t_sem, i_sem,
    up_send, down_send, z_recv, x_send, x_recv, y_send, y_recv, d_send, d_recv,
    s_send, s_recv, ex_send, ex_recv, ey_send, ey_recv, ed_send, ed_recv,
):
    depth, columns = rows.shape
    size = own.shape[1]
    frames = own.shape[1]
    per = slopes.shape[1] // own.shape[2]
    half = per // PARTS
    edge = TAIL // 2
    half_cols = columns // 2
    p = lax.axis_index("dp")
    b = lax.axis_index("blk")
    z, core = b // 2, b % 2
    sib = b + 1 - 2 * core
    across = (p + 1 - 2 * (p % 2), b)
    along = ((p + 2) % 4, b)
    beside = (p, sib)
    total_frames = 4 * frames

    lines = (own, xline, yline, dline)

    def chunk(line, zz, cc, h, cut=False):
        start = per - TAIL if h == PARTS else h * half
        count = TAIL if h == PARTS else half - (TAIL if cut else 0)
        return line.at[pl.ds((zz * 2 + cc) * per + start, count)]

    def piece(n, s, h):
        return h, n == 3 and s == depth_z - 1 and h == PARTS - 1

    def remote(src, dst, send, recv, to):
        return pltpu.make_async_remote_copy(
            src_ref=src, dst_ref=dst, send_sem=send, recv_sem=recv, device_id=to, device_id_type=MESH
        )

    def up(n, zz, h, cut=False):
        c = chunk(lines[n], zz, core, h, cut)
        return remote(c, c, up_send.at[n // 3, zz, h], z_recv.at[n // 3, zz, h], (p, b + 2))

    def down(n, zz, h, cut=False):
        c = chunk(lines[n], zz, core, h, cut)
        return remote(c, c, down_send.at[n // 3, zz, h], z_recv.at[n // 3, zz, h], (p, b - 2))

    def over_x(zz, h):
        return remote(chunk(own, zz, core, h), chunk(xline, zz, core, h), x_send.at[zz, h], x_recv.at[zz, h], across)

    def over_y(zz, h):
        return remote(chunk(own, zz, core, h), chunk(yline, zz, core, h), y_send.at[zz, h], y_recv.at[zz, h], along)

    def diagonal(zz, h):
        to = (across, along)[h % 2]
        source = turned.at[pl.ds(h * half, half)]
        return remote(source, chunk(dline, zz, core, h), d_send.at[zz, h], d_recv.at[zz, h], to)

    def corner(zz, i):
        source = turned.at[pl.ds(per + i * edge, edge)]
        target_ref = dline.at[pl.ds((zz * 2 + core + 1) * per - TAIL + i * edge, edge)]
        return remote(source, target_ref, d_send.at[zz, i], d_recv.at[zz, i], (across, along)[i])

    def turn(zz, h):
        source = (yline, xline)[h % 2]

        def one(i, carry):
            turned[h * half + i] = source[(zz * 2 + core) * per + h * half + i].T
            return carry

        lax.fori_loop(0, half, one, 0)

    def turn_corner(zz):
        for i in range(TAIL):
            source = (yline, xline)[i // edge]
            turned[per + i] = source[(zz * 2 + core + 1) * per - TAIL + i].T

    def share(n, zz, h, cut=False):
        c = chunk(lines[n], zz, core, h, cut)
        return remote(c, c, s_send.at[n, zz, h], s_recv.at[n, zz, h], beside)

    def shared(n, zz, h, cut=False):
        c = chunk(lines[n], zz, 1 - core, h, cut)
        return remote(c, c, s_send.at[n, zz, h], s_recv.at[n, zz, h], beside)

    def error_part(ref, h):
        return ref.at[pl.ds(h * half_cols, half_cols)]

    def errors_x(h):
        return remote(error_part(e0, h), error_part(ex, h), ex_send.at[h], ex_recv.at[h], across)

    def errors_y(h):
        return remote(error_part(e0, h), error_part(ey, h), ey_send.at[h], ey_recv.at[h], along)

    def errors_d(h):
        source, to = ((ey, across), (ex, along))[h]
        return remote(error_part(source, h), error_part(ed, h), ed_send.at[h], ed_recv.at[h], to)

    def load_weights(j):
        slot = j % SLOTS
        return pltpu.make_async_copy(weights.at[j], wbuf.at[slot], w_sem.at[slot])

    def load_target():
        return pltpu.make_async_copy(target, tbuf, t_sem)

    def load_tables():
        both = ((rows_in, rows), (live_in, live))
        return [pltpu.make_async_copy(a, b, i_sem.at[n]) for n, (a, b) in enumerate(both)]

    barrier = pltpu.get_barrier_semaphore()
    for to in (across, along, beside):
        pl.semaphore_signal(barrier, inc=1, device_id=to, device_id_type=MESH)

    @pl.when(z > 0)
    def _():
        pl.semaphore_signal(barrier, inc=1, device_id=(p, b - 2), device_id_type=MESH)

    @pl.when(z < depth_z - 1)
    def _():
        pl.semaphore_signal(barrier, inc=1, device_id=(p, b + 2), device_id_type=MESH)

    for i in range(per):
        pltpu.make_async_copy(
            slopes.at[:, pl.ds(i * size, size)], own.at[b * per + i], load_sem.at[i // half]
        ).start()

    pl.semaphore_wait(barrier, 3 + jnp.minimum(z, 1) + jnp.minimum(depth_z - 1 - z, 1))

    def at_distance(s, act):
        if s == 0:
            act(z, True, True)
            return

        @pl.when(z - s >= 0)
        def _():
            act(z - s, True, False)

        @pl.when(z + s < depth_z)
        def _():
            act(z + s, False, True)

    def relay(n, zz, h, s, upward, downward):
        if upward:
            @pl.when(z < depth_z - 1)
            def _():
                up(n, zz, *piece(n, s + 1, h)).start()
        if downward:
            @pl.when(z > 0)
            def _():
                down(n, zz, *piece(n, s + 1, h)).start()

    def send_own(s, h):
        def act(zz, upward, downward):
            if s > 0:
                (up if upward else down)(0, zz, h).wait_recv()
            relay(0, zz, h, s, upward, downward)
            share(0, zz, h).start()

        def spread(zz, upward, downward):
            over_x(zz, h).start()
            over_y(zz, h).start()

        at_distance(s, act)
        if s == 1:
            pass_on(0, h)
        at_distance(s, spread)

    def send_diagonal(s, h, inner):
        def act(zz, upward, downward):
            if s == 0:
                diagonal(zz, h).wait_recv()
                relay(3, zz, h, s, upward, downward)
                share(3, zz, h).start()
                return
            if s == depth_z - 1 and h == 0:
                for i in range(2):
                    corner(zz, i).wait_recv()
                share(3, zz, PARTS).start()
            (up if upward else down)(3, zz, *piece(3, s, h)).wait_recv()
            if s < depth_z - 1:
                relay(3, zz, h, s, upward, downward)
            share(3, zz, *piece(3, s, h)).start()

        def guarded(zz, upward, downward):
            ends = z < depth_z - 1 if upward else z > 0

            @pl.when(ends if inner else jnp.logical_not(ends))
            def _():
                act(zz, upward, downward)

        at_distance(s, act if s == 0 else guarded)

    def pass_on(s, h):
        def act(zz, upward, downward):
            over_x(zz, h).wait_recv()
            over_y(zz, h).wait_recv()
            if s == 0:
                turn(zz, h)
                diagonal(zz, h).start()
            if s == depth_z - 1 and h == PARTS - 1:
                turn_corner(zz)
                for i in range(2):
                    corner(zz, i).start()
            share(1, zz, h).start()
            share(2, zz, h).start()

        at_distance(s, act)

    for h in range(PARTS):
        pltpu.make_async_copy(chunk(own, z, core, h), chunk(own, z, core, h), load_sem.at[h]).wait()
        send_own(0, h)
    load_target().start()
    for copy in load_tables():
        copy.start()
    for j in range(SLOTS):
        load_weights(j).start()
    for s in range(1, depth_z):
        if s == depth_z - 1:
            for h in range(PARTS):
                send_diagonal(0, h, True)
        for h in range(PARTS):
            send_own(s, h)

    for zz in range(depth_z):
        for h in range(PARTS):
            shared(0, zz, h).wait_recv()
    load_target().wait()
    for copy in load_tables():
        copy.wait()

    def forward(j, carry):
        load_weights(j).wait()
        slot = j % SLOTS
        picked, masked = [], []
        for k in range(depth):
            picked.append(own[rows[k, j]])
            keep = jnp.full((size, size), live[k, j].astype(jnp.float32), jnp.float32).astype(jnp.bfloat16)
            masked.append(wbuf[slot, k] * keep)
        predicted = jnp.dot(
            jnp.concatenate(picked, 1), jnp.concatenate(masked, 0), preferred_element_type=jnp.float32
        )
        where = pl.ds(pl.multiple_of(j * size, size), size)
        phase[:, where] = predicted.astype(jnp.bfloat16)
        off = predicted - tbuf[:, where].astype(jnp.float32)
        e0[j] = (off * (1.0 / math.sqrt(total_frames))).astype(jnp.bfloat16)

        @pl.when(j + SLOTS < columns)
        def _():
            load_weights(j + SLOTS).start()

        return carry

    lax.fori_loop(0, columns, forward, 0)
    for h in range(2):
        errors_x(1 - h).start()
        errors_y(h).start()

    for s in range(1, depth_z):
        for h in range(PARTS):
            send_diagonal(s, h, True)
    for s in range(1, depth_z):
        for h in range(PARTS):
            pass_on(s, h)
    for s in range(1, depth_z - 1):
        if s == depth_z - 2:
            errors_y(0).wait_recv()
            errors_d(0).start()
            errors_x(1).wait_recv()
            errors_d(1).start()
        for h in range(PARTS):
            send_diagonal(s, h, False)
    errors_x(0).wait_recv()
    errors_y(1).wait_recv()
    for n in range(1, 3):
        for zz in range(depth_z):
            for h in range(PARTS):
                shared(n, zz, h).wait_recv()

    count = sums.shape[1] // size

    def near(j, carry):
        tiles = []
        for i in range(count):
            r = rows[p * count + i, j]
            tiles.append(jnp.concatenate([line[r] for line in (own, xline, yline)], 0))
        left = jnp.concatenate([e[j].T for e in (e0, ex, ey)], 1)
        both = jnp.dot(left, jnp.concatenate(tiles, 1), preferred_element_type=jnp.float32)
        for i in range(count):
            sums[j, pl.ds(i * size, size)] = both[:, i * size : (i + 1) * size].T
        return carry

    lax.fori_loop(0, columns, near, 0, unroll=2)

    def sent(lines_sent, ends):
        for h in range(PARTS):
            for s in range(depth_z):
                def done(zz, upward, downward, h=h, s=s):
                    for n in lines_sent:
                        if upward and n % 3 == 0 and s < depth_z - 1:
                            @pl.when(z < depth_z - 1)
                            def _(n=n):
                                up(n, zz, *piece(n, s + 1, h)).wait_send()
                        if downward and n % 3 == 0 and s < depth_z - 1:
                            @pl.when(z > 0)
                            def _(n=n):
                                down(n, zz, *piece(n, s + 1, h)).wait_send()
                        share(n, zz, *piece(n, s, h)).wait_send()
                        if n == 3 and s == depth_z - 1 and h == 0:
                            share(3, zz, PARTS).wait_send()
                    if not ends:
                        over_x(zz, h).wait_send()
                        over_y(zz, h).wait_send()
                        if s == 0:
                            diagonal(zz, h).wait_send()
                        if s == depth_z - 1 and h == 0:
                            for i in range(2):
                                corner(zz, i).wait_send()

                at_distance(s, done)

    sent((0, 1, 2), False)
    for h in range(PARTS):
        send_diagonal(depth_z - 1, h, False)
    for h in range(2):
        errors_x(h).wait_send()
        errors_y(h).wait_send()
        errors_d(h).wait_send()
        errors_d(h).wait_recv()
    for s in range(depth_z):
        for h in range(PARTS):
            def met(zz, upward, downward, s=s, h=h):
                shared(3, zz, *piece(3, s, h)).wait_recv()
                if s == depth_z - 1 and h == 0:
                    shared(3, zz, PARTS).wait_recv()

            at_distance(s, met)
    sent((3,), True)


def finish_kernel(phase, sums, dline, ed, rows, live, phase_out, grads_out, grads, phase_sem, grads_sem):
    columns, size, _ = ed.shape
    count = grads.shape[0]
    first = lax.axis_index("dp") * count
    pieces = grads_sem.shape[0]
    part = columns // pieces
    put = [pltpu.make_async_copy(phase, phase_out, phase_sem)]
    put[0].start()

    def far(j, carry):
        left = jnp.concatenate([dline[rows[first + i, j]] for i in range(count)], 0)
        both = sums[j] + jnp.dot(left, ed[j], preferred_element_type=jnp.float32)
        for i in range(count):
            keep = live[first + i, j].astype(jnp.float32)
            grads[i, j] = (both[i * size : (i + 1) * size] * keep).astype(jnp.bfloat16)
        return carry

    for q in range(pieces):
        lax.fori_loop(q * part, (q + 1) * part, far, 0, unroll=4)
        for i in range(count):
            where = (i, pl.ds(q * part, part))
            put.append(pltpu.make_async_copy(grads.at[where], grads_out.at[where], grads_sem.at[q, i]))
            put[-1].start()
    for copy in put:
        copy.wait()


def fused(slopes, weights, rows, live, target):
    frames = slopes.shape[0]
    columns, depth, size, _ = weights.shape
    blk = lax.axis_size("blk")
    depth_z = blk // 2
    blocks = slopes.shape[1] * blk // size
    count = depth // 4
    line = pltpu.VMEM((blocks, frames, size), jnp.bfloat16)
    errors = pltpu.VMEM((columns, frames, size), jnp.bfloat16)
    table = pltpu.SMEM((depth, columns), jnp.int32)
    dma = pltpu.SemaphoreType.DMA
    everywhere = pl.BlockSpec(memory_space=pl.ANY)
    smem = pl.BlockSpec(memory_space=pltpu.SMEM)
    vmem = pl.BlockSpec(memory_space=pltpu.VMEM)
    inputs = [pltpu.with_memory_space_constraint(a, pltpu.HBM) for a in (slopes, weights, target, rows.T, live.T)]
    handed = pl.pallas_call(
        functools.partial(fused_kernel, depth_z),
        out_shape=(
            pltpu.VMEM(target.shape, jnp.bfloat16),
            pltpu.VMEM((columns, count * size, size), jnp.float32),
            line,
            errors,
            table,
            table,
        ),
        in_specs=[everywhere] * 5,
        out_specs=(vmem,) * 4 + (smem,) * 2,
        scratch_shapes=[line] * 3
        + [pltpu.VMEM((blocks // blk + TAIL, size, frames), jnp.bfloat16)]
        + [errors] * 3
        + [pltpu.VMEM((SLOTS, depth, size, size), jnp.bfloat16), pltpu.VMEM(target.shape, jnp.bfloat16)]
        + [dma((PARTS,)), dma((SLOTS,)), dma, dma((2,))]
        + [dma((2, depth_z, PARTS + 1))] * 3
        + [dma((depth_z, PARTS))] * 6
        + [dma((4, depth_z, PARTS + 1))] * 2
        + [dma((2,))] * 6,
        compiler_params=pltpu.CompilerParams(
            collective_id=0, has_side_effects=True, vmem_limit_bytes=VMEM_BYTES * 5 // 8
        ),
    )(*inputs)
    spaces = [pltpu.VMEM] * 4 + [pltpu.SMEM] * 2
    handed = [pltpu.with_memory_space_constraint(a, m) for a, m in zip(handed, spaces)]
    grads = (count, columns, size, size)
    return pl.pallas_call(
        finish_kernel,
        out_shape=(jax.ShapeDtypeStruct(target.shape, jnp.bfloat16), jax.ShapeDtypeStruct(grads, jnp.bfloat16)),
        in_specs=[vmem] * 4 + [smem] * 2,
        out_specs=(everywhere,) * 2,
        scratch_shapes=[pltpu.VMEM(grads, jnp.bfloat16), dma, dma((PIECES, count))],
        compiler_params=pltpu.CompilerParams(vmem_limit_bytes=VMEM_BYTES // 4),
    )(*handed)


def gathered_step(slopes, weights, rows, live, target):
    own = lax.all_gather(slopes, "blk", axis=1, tiled=True)
    everyone = lax.all_gather(own, "dp", axis=0, tiled=True)
    frames = own.shape[0]
    columns, depth, size, _ = weights.shape
    dp = lax.axis_size("dp")
    share = depth // dp
    total_frames = frames * dp

    def tiles(lines, some):
        return [lax.dynamic_slice_in_dim(lines, some[k] * size, size, 1) for k in range(some.shape[0])]

    def forward(column):
        blocks, some, seen = column
        masked = blocks * seen.astype(jnp.bfloat16)[:, None, None]
        return jnp.dot(
            jnp.concatenate(tiles(own, some), 1), masked.reshape(-1, size), preferred_element_type=jnp.float32
        )

    predicted = jnp.transpose(lax.map(forward, (weights, rows, live)), (1, 0, 2)).reshape(frames, -1)
    errors = ((predicted - target.astype(jnp.float32)) * (1.0 / math.sqrt(total_frames))).astype(jnp.bfloat16)
    errors = lax.all_gather(errors, "dp", axis=0, tiled=True)
    first = lax.axis_index("dp") * share

    def backward(column):
        j, some, seen = column
        left = jnp.concatenate(tiles(everyone, some), 1)
        right = lax.dynamic_slice_in_dim(errors, j * size, size, 1)
        grads = lax.dot_general(left, right, (((0,), (0,)), ((), ())), preferred_element_type=jnp.float32)
        return (grads.reshape(share, size, size) * seen.astype(jnp.float32)[:, None, None]).astype(jnp.bfloat16)

    mine = [lax.dynamic_slice_in_dim(a, first, share, 1) for a in (rows, live)]
    grads = lax.map(backward, (jnp.arange(columns), *mine))
    return predicted.astype(jnp.bfloat16), jnp.transpose(grads, (1, 0, 2, 3))


def on_device(slopes, weights, rows, live, target):
    dp, blk = lax.axis_size("dp"), lax.axis_size("blk")
    held = 2 * dp * slopes.size * blk + 6 * target.size * dp
    if dp == 4 and blk == 8 and slopes.shape[0] == weights.shape[2] and held < VMEM_BYTES * 3 // 4:
        return fused(slopes, weights, rows, live, target)
    return gathered_step(slopes, weights, rows, live, target)


def solution(mesh):
    return jax.shard_map(
        on_device,
        mesh=mesh,
        in_specs=(
            P("dp", "blk"),
            P("blk", None, None, None),
            P("blk", None),
            P("blk", None),
            P("dp", "blk"),
        ),
        out_specs=(P("dp", "blk"), P("dp", "blk", None, None)),
        check_vma=False,
    )
```

```python
import functools
import math

import jax
import jax.numpy as jnp
from jax import lax
from jax.experimental import pallas as pl
from jax.experimental.pallas import tpu as pltpu
from jax.sharding import PartitionSpec as P

MESH = pl.DeviceIdType.MESH
VMEM_BYTES = 64 << 20
SLOTS = 4
PARTS = 2
TAIL = 2
WHOLE = -1
PIECES = 8


def fused_kernel(
    depth_z, slopes, weights, target, rows_in, live_in, phase, sums, dline, ed, rows, live,
    own, xline, yline, turned, e0, ex, ey, wbuf, tbuf, load_sem, w_sem, t_sem, i_sem,
    up_send, down_send, z_recv, x_send, x_recv, y_send, y_recv, d_send, d_recv,
    s_send, s_recv, ex_send, ex_recv, ey_send, ey_recv, ed_send, ed_recv,
):
    depth, columns = rows.shape
    size = own.shape[1]
    frames = own.shape[1]
    per = slopes.shape[1] // own.shape[2]
    half = per // PARTS
    edge = TAIL // 2
    half_cols = columns // 2
    p = lax.axis_index("dp")
    b = lax.axis_index("blk")
    z, core = b // 2, b % 2
    sib = b + 1 - 2 * core
    across = (p + 1 - 2 * (p % 2), b)
    along = ((p + 2) % 4, b)
    beside = (p, sib)
    total_frames = 4 * frames

    lines = (own, xline, yline, dline)

    def chunk(line, zz, cc, h, cut=False):
        if h == WHOLE:
            start, count = 0, per
        elif h == PARTS:
            start, count = per - TAIL, TAIL
        else:
            start, count = h * half, half - (TAIL if cut else 0)
        return line.at[pl.ds((zz * 2 + cc) * per + start, count)]

    def piece(n, s, h):
        return h, n == 3 and s == depth_z - 1 and h == PARTS - 1

    def remote(src, dst, send, recv, to):
        return pltpu.make_async_remote_copy(
            src_ref=src, dst_ref=dst, send_sem=send, recv_sem=recv, device_id=to, device_id_type=MESH
        )

    def up(n, zz, h, cut=False):
        c = chunk(lines[n], zz, core, h, cut)
        return remote(c, c, up_send.at[n // 3], z_recv.at[n // 3, zz, h], (p, b + 2))

    def down(n, zz, h, cut=False):
        c = chunk(lines[n], zz, core, h, cut)
        return remote(c, c, down_send.at[n // 3], z_recv.at[n // 3, zz, h], (p, b - 2))

    def over_x(zz, h):
        return remote(chunk(own, zz, core, h), chunk(xline, zz, core, h), x_send, x_recv.at[zz, h], across)

    def over_y(zz, h):
        return remote(chunk(own, zz, core, h), chunk(yline, zz, core, h), y_send, y_recv.at[zz, h], along)

    def diagonal(zz, h):
        to = (across, along)[h % 2]
        source = turned.at[pl.ds(h * half, half)]
        return remote(source, chunk(dline, zz, core, h), d_send.at[h], d_recv.at[h], to)

    def corner(zz, i):
        source = turned.at[pl.ds(per + i * edge, edge)]
        target_ref = dline.at[pl.ds((zz * 2 + core + 1) * per - TAIL + i * edge, edge)]
        return remote(source, target_ref, d_send.at[PARTS + i], d_recv.at[PARTS + i], (across, along)[i])

    def turn(zz, h):
        source = (yline, xline)[h % 2]

        def one(i, carry):
            turned[h * half + i] = source[(zz * 2 + core) * per + h * half + i].T
            return carry

        lax.fori_loop(0, half, one, 0)

    def turn_corner(zz):
        for i in range(TAIL):
            source = (yline, xline)[i // edge]
            turned[per + i] = source[(zz * 2 + core + 1) * per - TAIL + i].T

    def share(n, zz, h, cut=False):
        c = chunk(lines[n], zz, core, h, cut)
        return remote(c, c, s_send.at[n], s_recv.at[n], beside)

    def many(n, count, send, recv):
        c = lines[n].at[pl.ds(0, count)]
        return remote(c, c, send, recv, beside)

    def shared(n):
        return many(n, depth_z * per, s_send.at[n], s_recv.at[n])

    def error_part(ref, h):
        return ref.at[pl.ds(h * half_cols, half_cols)]

    def errors_x(h):
        return remote(error_part(e0, h), error_part(ex, h), ex_send, ex_recv.at[h], across)

    def errors_y(h):
        return remote(error_part(e0, h), error_part(ey, h), ey_send, ey_recv.at[h], along)

    def errors_d(h):
        source, to = ((ey, across), (ex, along))[h]
        return remote(error_part(source, h), error_part(ed, h), ed_send, ed_recv.at[h], to)

    def load_weights(j):
        slot = j % SLOTS
        return pltpu.make_async_copy(weights.at[j], wbuf.at[slot], w_sem.at[slot])

    def load_target():
        return pltpu.make_async_copy(target, tbuf, t_sem)

    def load_tables():
        both = ((rows_in, rows), (live_in, live))
        return [pltpu.make_async_copy(a, b, i_sem.at[n]) for n, (a, b) in enumerate(both)]

    barrier = pltpu.get_barrier_semaphore()
    for to in (across, along, beside):
        pl.semaphore_signal(barrier, inc=1, device_id=to, device_id_type=MESH)

    @pl.when(z > 0)
    def _():
        pl.semaphore_signal(barrier, inc=1, device_id=(p, b - 2), device_id_type=MESH)

    @pl.when(z < depth_z - 1)
    def _():
        pl.semaphore_signal(barrier, inc=1, device_id=(p, b + 2), device_id_type=MESH)

    for i in range(per):
        pltpu.make_async_copy(
            slopes.at[:, pl.ds(i * size, size)], own.at[b * per + i], load_sem.at[i // half]
        ).start()

    pl.semaphore_wait(barrier, 3 + jnp.minimum(z, 1) + jnp.minimum(depth_z - 1 - z, 1))

    def at_distance(s, act):
        if s == 0:
            act(z, True, True)
            return

        @pl.when(z - s >= 0)
        def _():
            act(z - s, True, False)

        @pl.when(z + s < depth_z)
        def _():
            act(z + s, False, True)

    def relay(n, zz, h, s, upward, downward):
        if upward:
            @pl.when(z < depth_z - 1)
            def _():
                up(n, zz, *piece(n, s + 1, h)).start()
        if downward:
            @pl.when(z > 0)
            def _():
                down(n, zz, *piece(n, s + 1, h)).start()

    def send_own(s, h):
        def act(zz, upward, downward):
            if s > 0:
                (up if upward else down)(0, zz, h).wait_recv()
            relay(0, zz, h, s, upward, downward)
            share(0, zz, h).start()

        def spread(zz, upward, downward):
            over_x(zz, h).start()
            over_y(zz, h).start()

        at_distance(s, act)
        if s == 1:
            pass_on(0, h)
        at_distance(s, spread)

    def send_diagonal(s, h, inner):
        def act(zz, upward, downward):
            if s == 0:
                diagonal(zz, h).wait_recv()
                relay(3, zz, h, s, upward, downward)
                share(3, zz, h).start()
                return
            if s == depth_z - 1 and h == 0:
                for i in range(2):
                    corner(zz, i).wait_recv()
                share(3, zz, PARTS).start()
            (up if upward else down)(3, zz, *piece(3, s, h)).wait_recv()
            if s < depth_z - 1:
                relay(3, zz, h, s, upward, downward)
            share(3, zz, *piece(3, s, h)).start()

        def guarded(zz, upward, downward):
            ends = z < depth_z - 1 if upward else z > 0

            @pl.when(ends if inner else jnp.logical_not(ends))
            def _():
                act(zz, upward, downward)

        at_distance(s, act if s == 0 else guarded)

    def pass_on(s, h):
        def act(zz, upward, downward):
            over_x(zz, h).wait_recv()
            over_y(zz, h).wait_recv()
            if s == 0:
                turn(zz, h)
                diagonal(zz, h).start()
            if s == depth_z - 1 and h == PARTS - 1:
                turn_corner(zz)
                for i in range(2):
                    corner(zz, i).start()
            share(1, zz, h).start()
            share(2, zz, h).start()

        at_distance(s, act)

    for h in range(PARTS):
        pltpu.make_async_copy(chunk(own, z, core, h), chunk(own, z, core, h), load_sem.at[h]).wait()
        send_own(0, h)
    load_target().start()
    for copy in load_tables():
        copy.start()
    for j in range(SLOTS):
        load_weights(j).start()
    for s in range(1, depth_z):
        if s == depth_z - 1:
            for h in range(PARTS):
                send_diagonal(0, h, True)
        for h in range(PARTS):
            send_own(s, h)

    shared(0).wait_recv()
    load_target().wait()
    for copy in load_tables():
        copy.wait()

    def forward(j, carry):
        load_weights(j).wait()
        slot = j % SLOTS
        picked, masked = [], []
        for k in range(depth):
            picked.append(own[rows[k, j]])
            keep = jnp.full((size, size), live[k, j].astype(jnp.float32), jnp.float32).astype(jnp.bfloat16)
            masked.append(wbuf[slot, k] * keep)
        predicted = jnp.dot(
            jnp.concatenate(picked, 1), jnp.concatenate(masked, 0), preferred_element_type=jnp.float32
        )
        where = pl.ds(pl.multiple_of(j * size, size), size)
        phase[:, where] = predicted.astype(jnp.bfloat16)
        off = predicted - tbuf[:, where].astype(jnp.float32)
        e0[j] = (off * (1.0 / math.sqrt(total_frames))).astype(jnp.bfloat16)

        @pl.when(j + SLOTS < columns)
        def _():
            load_weights(j + SLOTS).start()

        return carry

    lax.fori_loop(0, columns, forward, 0)
    for h in range(2):
        errors_x(1 - h).start()
        errors_y(h).start()

    for s in range(1, depth_z):
        for h in range(PARTS):
            send_diagonal(s, h, True)
    for s in range(1, depth_z):
        for h in range(PARTS):
            pass_on(s, h)
    for s in range(1, depth_z - 1):
        if s == depth_z - 2:
            errors_y(0).wait_recv()
            errors_d(0).start()
            errors_x(1).wait_recv()
            errors_d(1).start()
        for h in range(PARTS):
            send_diagonal(s, h, False)
    errors_x(0).wait_recv()
    errors_y(1).wait_recv()
    for n in range(1, 3):
        shared(n).wait_recv()

    count = sums.shape[1] // size

    def near(j, carry):
        tiles = []
        for i in range(count):
            r = rows[p * count + i, j]
            tiles.append(jnp.concatenate([line[r] for line in (own, xline, yline)], 0))
        left = jnp.concatenate([e[j].T for e in (e0, ex, ey)], 1)
        both = jnp.dot(left, jnp.concatenate(tiles, 1), preferred_element_type=jnp.float32)
        for i in range(count):
            sums[j, pl.ds(i * size, size)] = both[:, i * size : (i + 1) * size].T
        return carry

    lax.fori_loop(0, columns, near, 0, unroll=2)

    def relayed(n):
        for here in range(depth_z):
            @pl.when(z == here)
            def _(here=here):
                if here < depth_z - 1:
                    count = (here + 1) * per - (TAIL if n == 3 and here == depth_z - 2 else 0)
                    many(n, count, up_send.at[n // 3], s_recv.at[n]).wait_send()
                if here > 0:
                    count = (depth_z - here) * per - (TAIL if n == 3 and here == 1 else 0)
                    many(n, count, down_send.at[n // 3], s_recv.at[n]).wait_send()

    relayed(0)
    relayed(3)
    for n in range(3):
        shared(n).wait_send()
    for send in (x_send, y_send):
        many(0, depth_z * per, send, s_recv.at[0]).wait_send()
    for h in range(PARTS):
        diagonal(z, h).wait_send()

    def corners_sent(zz, upward, downward):
        for i in range(2):
            corner(zz, i).wait_send()

    at_distance(depth_z - 1, corners_sent)
    for h in range(PARTS):
        send_diagonal(depth_z - 1, h, False)
    for h in range(2):
        errors_d(h).wait_recv()
    for send in (ex_send, ey_send, ed_send):
        remote(e0, e0, send, ex_recv.at[0], beside).wait_send()
    shared(3).wait_recv()
    shared(3).wait_send()


def finish_kernel(phase, sums, dline, ed, rows, live, phase_out, grads_out, grads, phase_sem, grads_sem):
    columns, size, _ = ed.shape
    count = grads.shape[0]
    first = lax.axis_index("dp") * count
    part = columns // PIECES
    put_phase = pltpu.make_async_copy(phase, phase_out, phase_sem)
    put_phase.start()

    def far(j, carry):
        left = jnp.concatenate([dline[rows[first + i, j]] for i in range(count)], 0)
        both = sums[j] + jnp.dot(left, ed[j], preferred_element_type=jnp.float32)
        for i in range(count):
            keep = live[first + i, j].astype(jnp.float32)
            grads[i, j] = (both[i * size : (i + 1) * size] * keep).astype(jnp.bfloat16)
        return carry

    for q in range(PIECES):
        lax.fori_loop(q * part, (q + 1) * part, far, 0, unroll=4)
        for i in range(count):
            where = (i, pl.ds(q * part, part))
            pltpu.make_async_copy(grads.at[where], grads_out.at[where], grads_sem).start()
    put_phase.wait()
    pltpu.make_async_copy(grads, grads_out, grads_sem).wait()


def fused(slopes, weights, rows, live, target):
    frames = slopes.shape[0]
    columns, depth, size, _ = weights.shape
    blk = lax.axis_size("blk")
    depth_z = blk // 2
    blocks = slopes.shape[1] * blk // size
    count = depth // 4
    line = pltpu.VMEM((blocks, frames, size), jnp.bfloat16)
    errors = pltpu.VMEM((columns, frames, size), jnp.bfloat16)
    table = pltpu.SMEM((depth, columns), jnp.int32)
    dma = pltpu.SemaphoreType.DMA
    everywhere = pl.BlockSpec(memory_space=pl.ANY)
    smem = pl.BlockSpec(memory_space=pltpu.SMEM)
    vmem = pl.BlockSpec(memory_space=pltpu.VMEM)
    inputs = [pltpu.with_memory_space_constraint(a, pltpu.HBM) for a in (slopes, weights, target, rows.T, live.T)]
    handed = pl.pallas_call(
        functools.partial(fused_kernel, depth_z),
        out_shape=(
            pltpu.VMEM(target.shape, jnp.bfloat16),
            pltpu.VMEM((columns, count * size, size), jnp.float32),
            line,
            errors,
            table,
            table,
        ),
        in_specs=[everywhere] * 5,
        out_specs=(vmem,) * 4 + (smem,) * 2,
        scratch_shapes=[line] * 3
        + [pltpu.VMEM((blocks // blk + TAIL, size, frames), jnp.bfloat16)]
        + [errors] * 3
        + [pltpu.VMEM((SLOTS, depth, size, size), jnp.bfloat16), pltpu.VMEM(target.shape, jnp.bfloat16)]
        + [dma((PARTS,)), dma((SLOTS,)), dma, dma((2,))]
        + [dma((2,)), dma((2,)), dma((2, depth_z, PARTS))]
        + [dma, dma((depth_z, PARTS))] * 2
        + [dma((PARTS + 2,))] * 2
        + [dma((4,))] * 2
        + [dma, dma((2,))] * 3,
        compiler_params=pltpu.CompilerParams(
            collective_id=0, has_side_effects=True, vmem_limit_bytes=VMEM_BYTES * 5 // 8
        ),
    )(*inputs)
    spaces = [pltpu.VMEM] * 4 + [pltpu.SMEM] * 2
    handed = [pltpu.with_memory_space_constraint(a, m) for a, m in zip(handed, spaces)]
    grads = (count, columns, size, size)
    return pl.pallas_call(
        finish_kernel,
        out_shape=(jax.ShapeDtypeStruct(target.shape, jnp.bfloat16), jax.ShapeDtypeStruct(grads, jnp.bfloat16)),
        in_specs=[vmem] * 4 + [smem] * 2,
        out_specs=(everywhere,) * 2,
        scratch_shapes=[pltpu.VMEM(grads, jnp.bfloat16), dma, dma],
        compiler_params=pltpu.CompilerParams(vmem_limit_bytes=VMEM_BYTES // 4),
    )(*handed)


def gathered_step(slopes, weights, rows, live, target):
    own = lax.all_gather(slopes, "blk", axis=1, tiled=True)
    everyone = lax.all_gather(own, "dp", axis=0, tiled=True)
    frames = own.shape[0]
    columns, depth, size, _ = weights.shape
    dp = lax.axis_size("dp")
    share = depth // dp
    total_frames = frames * dp

    def tiles(lines, some):
        return [lax.dynamic_slice_in_dim(lines, some[k] * size, size, 1) for k in range(some.shape[0])]

    def forward(column):
        blocks, some, seen = column
        masked = blocks * seen.astype(jnp.bfloat16)[:, None, None]
        return jnp.dot(
            jnp.concatenate(tiles(own, some), 1), masked.reshape(-1, size), preferred_element_type=jnp.float32
        )

    predicted = jnp.transpose(lax.map(forward, (weights, rows, live)), (1, 0, 2)).reshape(frames, -1)
    errors = ((predicted - target.astype(jnp.float32)) * (1.0 / math.sqrt(total_frames))).astype(jnp.bfloat16)
    errors = lax.all_gather(errors, "dp", axis=0, tiled=True)
    first = lax.axis_index("dp") * share

    def backward(column):
        j, some, seen = column
        left = jnp.concatenate(tiles(everyone, some), 1)
        right = lax.dynamic_slice_in_dim(errors, j * size, size, 1)
        grads = lax.dot_general(left, right, (((0,), (0,)), ((), ())), preferred_element_type=jnp.float32)
        return (grads.reshape(share, size, size) * seen.astype(jnp.float32)[:, None, None]).astype(jnp.bfloat16)

    mine = [lax.dynamic_slice_in_dim(a, first, share, 1) for a in (rows, live)]
    grads = lax.map(backward, (jnp.arange(columns), *mine))
    return predicted.astype(jnp.bfloat16), jnp.transpose(grads, (1, 0, 2, 3))


def on_device(slopes, weights, rows, live, target):
    dp, blk = lax.axis_size("dp"), lax.axis_size("blk")
    held = 2 * dp * slopes.size * blk + 6 * target.size * dp
    if dp == 4 and blk == 8 and slopes.shape[0] == weights.shape[2] and held < VMEM_BYTES * 3 // 4:
        return fused(slopes, weights, rows, live, target)
    return gathered_step(slopes, weights, rows, live, target)


def solution(mesh):
    return jax.shard_map(
        on_device,
        mesh=mesh,
        in_specs=(
            P("dp", "blk"),
            P("blk", None, None, None),
            P("blk", None),
            P("blk", None),
            P("dp", "blk"),
        ),
        out_specs=(P("dp", "blk"), P("dp", "blk", None, None)),
        check_vma=False,
    )
```
